32 devices in a mesh: pair: 2 (over x), grow: 4 (over y, core), gcol: 4 (over z).
Axes of the slice: x: 2, y: 2, z: 4, core: 2. Of those that a mesh axis runs over, the one named last changes fastest.
Arguments:
- core_matrix: bfloat16 [12288, 12288], P('grow', 'gcol'), may hold values from -0.00048828125 to 0.00048828125
- pair_panels: bfloat16 [12, 32, 12288], P('pair', None, ('grow', 'gcol')), may hold values from -6 to 6
- amplitudes: bfloat16 [12, 32, 32], P('pair'), may hold values from -0.1875 to 0.1875
- pair_widths: int32 [12], P('pair'), may hold values from 8 to 32
- batch_plan: int32 [12], P('pair'), may hold values from 0 to 11, each once
Outputs:
- residual: float32 [12, 1024], P('pair', ('grow', 'gcol'))
The draws below stay inside these ranges and needn't reach their ends.
Inputs may be any that keep to these rules, and one draw needn't show every extreme that they name: batch_plan names every pair exactly once.
All inputs are finite; a program needn't handle non-finite values.
Results may differ from the reference program's by a relative error of at most 0.015.
Values may be sent and summed in bfloat16 or wider, within the bound.
A program may use at most 64 MiB of HBM per device.

```python
import jax
import jax.numpy as jnp
from jax import lax

NG = 12288
NPNO = 32
PAIRS = 12


def set_ends(drawn, key, low, top_value):
    longest = drawn.shape.index(max(drawn.shape))
    spots = []
    for shift in (0, 1):
        where = [jax.random.randint(jax.random.fold_in(key, axis), (), 0, length) for axis, length in enumerate(drawn.shape)]
        where[longest] = (where[longest] + shift) % drawn.shape[longest]
        spots.append(tuple(where))
    return drawn.at[spots[0]].set(low).at[spots[1]].set(top_value)


def shard_levels(rng, dims, split, smallest, high):
    factor_of = 1.0
    for axis_at, shards_of in split:
        draws = jax.random.uniform(jax.random.fold_in(jax.random.fold_in(rng, 6), axis_at), (shards_of,), jnp.float32, smallest / len(split), high / len(split))
        factor_of = factor_of * jnp.repeat(jnp.exp(draws), dims[axis_at] // shards_of).reshape((-1,) + (1,) * (len(dims) - 1 - axis_at))
    return factor_of


def gaussian(own_key, shape, scale, reach, shards=(), kind=jnp.bfloat16):
    drawn = scale * jax.random.normal(own_key, shape, jnp.float32)
    if shards:
        drawn = drawn * shard_levels(own_key, shape, shards, -0.22, 0.18)
    return jnp.clip(drawn, -reach, reach).astype(kind)


def setup_inputs(seed: int = 0) -> dict:
    splits = jax.random.split(jax.random.key(seed), 6)
    return {
        "core_matrix": gaussian(splits[0], (NG, NG), (NG * NG) ** -0.5, 0.00048828125, ((0, 4), (1, 4))),
        "pair_panels": gaussian(splits[1], (PAIRS, NPNO, NG), 1.0, 6.0, ((0, 2), (2, 16))),
        "amplitudes": gaussian(splits[2], (PAIRS, NPNO, NPNO), (NPNO * NPNO) ** -0.5, 0.1875, ((0, 2),)),
        "pair_widths": set_ends(jax.random.randint(splits[3], (PAIRS,), NPNO // 4, NPNO + 1), jax.random.fold_in(splits[3], 1), NPNO // 4, NPNO).astype(jnp.int32),
        "batch_plan": jax.random.permutation(splits[4], PAIRS).astype(jnp.int32),
    }


def pair_term(core_matrix, panel, amps, width):
    live = (lax.iota(jnp.int32, NPNO) < width).astype(jnp.bfloat16)
    masked = amps * live[:, None] * live[None, :]
    projected = jnp.dot(masked, panel, preferred_element_type=jnp.float32).astype(jnp.bfloat16)
    block = min(512, NG)
    count = NG // block

    def step(total, which):
        start = (which * block).astype(jnp.int32)
        left = lax.dynamic_slice_in_dim(panel, start, block, 1)
        core_rows = lax.dynamic_slice_in_dim(core_matrix, start, block, 0)
        coupled = lax.dot_general(left, projected, (((0,), (0,)), ((), ())), preferred_element_type=jnp.float32).astype(jnp.bfloat16)
        coupled = lax.optimization_barrier(coupled)
        weighted = (core_rows.astype(jnp.float32) * coupled.astype(jnp.float32)).astype(jnp.bfloat16)
        back = lax.dot_general(weighted, panel, (((1,), (1,)), ((), ())), preferred_element_type=jnp.float32).astype(jnp.bfloat16)
        total = total + jnp.dot(left, back, preferred_element_type=jnp.float32)
        return total, None

    total, _ = lax.scan(step, jnp.zeros((NPNO, NPNO), jnp.float32), jnp.arange(count, dtype=jnp.int32))
    keep = live.astype(jnp.float32)
    return (total * keep[:, None] * keep[None, :]).reshape(NPNO * NPNO)


def reference(core_matrix, pair_panels, amplitudes, pair_widths, batch_plan):
    def single(pair_id):
        return pair_term(core_matrix, pair_panels[pair_id], amplitudes[pair_id], pair_widths[pair_id])

    return lax.map(single, batch_plan)
```

```python
import functools

import jax
import jax.numpy as jnp
from jax import lax
from jax.experimental import pallas as pl
from jax.experimental.pallas import tpu as pltpu
from jax.sharding import PartitionSpec as P

MESH = pl.DeviceIdType.MESH
TILE = 512
CHUNK = 256
F32 = jnp.float32
BF16 = jnp.bfloat16


def gather_kernel(ngrow, ngcol, panel_ref, left_ref, right_ref, lsend, lrecv, rsend, rrecv, own_sem):
    x, g, c = lax.axis_index("pair"), lax.axis_index("grow"), lax.axis_index("gcol")
    piece = panel_ref.shape[2]
    index = g * ngcol + c
    column = lax.div(index, ngrow)
    slot = lax.rem(index, ngrow)
    self_in = jnp.where(column == c, 1, 0)

    barrier = pltpu.get_barrier_semaphore()

    def greet(device):
        pl.semaphore_signal(barrier, inc=1, device_id=device, device_id_type=MESH)

    def right_source(k):
        j = lax.rem(slot + k, ngrow)
        i = c * ngrow + j
        return j, lax.div(i, ngcol), lax.rem(i, ngcol)

    for k in range(1, ngcol):
        greet((x, g, lax.rem(c + k, ngcol)))
    for k in range(ngrow):
        gt = lax.rem(g + k, ngrow)

        @pl.when(jnp.logical_or(gt != g, column != c))
        def _():
            greet((x, gt, column))

        _, gs, cs = right_source(k)

        @pl.when(jnp.logical_or(gs != g, cs != c))
        def _():
            greet((x, gs, cs))

    pl.semaphore_wait(barrier, ngcol - 1 + 2 * (ngrow - self_in))

    def spot(ref, at):
        return ref.at[:, :, pl.ds(pl.multiple_of(at * piece, 128), piece)]

    def left_copy(k):
        return pltpu.make_async_remote_copy(
            src_ref=panel_ref, dst_ref=spot(left_ref, c), send_sem=lsend.at[k], recv_sem=lrecv.at[k],
            device_id=(x, g, lax.rem(c + k, ngcol)), device_id_type=MESH)

    def right_copy(k):
        return pltpu.make_async_remote_copy(
            src_ref=panel_ref, dst_ref=spot(right_ref, slot), send_sem=rsend.at[k], recv_sem=rrecv.at[slot],
            device_id=(x, lax.rem(g + k, ngrow), column), device_id_type=MESH)

    for k in range(1, ngcol):
        left_copy(k).start()
    for k in range(1, ngrow):
        right_copy(k).start()

    @pl.when(self_in == 0)
    def _():
        right_copy(0).start()

    own_left = pltpu.make_async_copy(panel_ref, spot(left_ref, c), own_sem.at[0])
    own_right = pltpu.make_async_copy(panel_ref, spot(right_ref, slot), own_sem.at[1])
    own_left.start()

    @pl.when(self_in == 1)
    def _():
        own_right.start()
        own_right.wait()

    own_left.wait()
    for k in range(1, ngcol):
        source = lax.rem(c + ngcol - k, ngcol)
        pltpu.make_async_remote_copy(
            src_ref=panel_ref, dst_ref=spot(left_ref, source), send_sem=lsend.at[k], recv_sem=lrecv.at[k],
            device_id=(x, g, lax.rem(c + k, ngcol)), device_id_type=MESH).wait_recv()
        left_copy(k).wait_send()
    for k in range(ngrow):
        j, gs, cs = right_source(k)

        @pl.when(jnp.logical_or(gs != g, cs != c))
        def _():
            pltpu.make_async_remote_copy(
                src_ref=panel_ref, dst_ref=spot(right_ref, j), send_sem=rsend.at[k], recv_sem=rrecv.at[j],
                device_id=(x, gs, cs), device_id_type=MESH).wait_recv()

    for k in range(1, ngrow):
        right_copy(k).wait_send()

    @pl.when(self_in == 0)
    def _():
        right_copy(0).wait_send()


def term_kernel(widths, left_ref, amps_ref, right_ref, core_ref, out_ref, y_ref, x_ref, v_ref, p_ref, g_ref, lad_ref):
    step = pl.program_id(0)
    npair, depth, _ = left_ref.shape
    groups = depth // 8

    def half_width(p):
        return lax.div(widths[p] + 1, 2)

    def rows_of(count):
        full = lax.div(count, 4)
        return 16 * (2 * full * (full + 1) + lax.rem(count, 4) * (full + 1))

    def each_duo(p, offset, body):
        count = half_width(p)
        for group in range(groups):
            low = 4 * group

            def run(duo, carry, group=group, low=low):
                base = offset + 16 * (2 * group * (group + 1) + (duo - low) * (group + 1))
                body(group, 2 * duo, pl.multiple_of(base, 16))
                return carry

            lax.fori_loop(low, jnp.clip(count, low, low + 4), run, 0)

    @pl.when(step == 0)
    def _():
        lad_ref[...] = jnp.zeros_like(lad_ref)

        def build(p, offset):
            x_ref[...] = left_ref[p].astype(F32)

            def duo(group, a, base):
                first, second = x_ref[pl.ds(a, 1), :], x_ref[pl.ds(a + 1, 1), :]
                for other in range(group + 1):
                    block = x_ref[8 * other : 8 * other + 8, :]
                    both = jnp.concatenate([first * block, second * block], axis=0)
                    y_ref[pl.ds(base + 16 * other, 16), :] = both.astype(BF16)

            each_duo(p, offset, duo)
            return offset + rows_of(half_width(p))

        lax.fori_loop(0, npair, build, jnp.int32(0))

    total = jnp.int32(0)
    for p in range(npair):
        total += rows_of(half_width(p))

    def multiply(i, carry):
        rows = pl.ds(pl.multiple_of(i * CHUNK, CHUNK), CHUNK)
        v_ref[rows, :] = jnp.dot(y_ref[rows, :], core_ref[...], preferred_element_type=F32)
        return carry

    lax.fori_loop(0, lax.div(total + CHUNK - 1, CHUNK), multiply, 0)

    def fold(p, offset):
        width = widths[p]
        live = jnp.logical_and(
            lax.broadcasted_iota(jnp.int32, (depth, depth), 0) < width,
            lax.broadcasted_iota(jnp.int32, (depth, depth), 1) < width)
        masked = jnp.where(live, amps_ref[p].astype(F32), 0.0).astype(BF16)
        right = right_ref[p]
        p_ref[...] = jnp.dot(masked, right, preferred_element_type=F32).astype(BF16).astype(F32)
        g_ref[...] = jnp.zeros_like(g_ref)

        def duo(group, a, base):
            first, second = p_ref[pl.ds(a, 1), :], p_ref[pl.ds(a + 1, 1), :]
            sum0 = sum1 = None
            for other in range(group + 1):
                upper = v_ref[pl.ds(base + 16 * other, 8), :]
                lower = v_ref[pl.ds(base + 16 * other + 8, 8), :]
                proj = p_ref[8 * other : 8 * other + 8, :]
                sum0 = upper * proj if sum0 is None else sum0 + upper * proj
                sum1 = lower * proj if sum1 is None else sum1 + lower * proj
                if other < group:
                    g_ref[8 * other : 8 * other + 8, :] += upper * first + lower * second
            g_ref[pl.ds(a, 1), :] += jnp.sum(sum0, axis=0, keepdims=True)
            g_ref[pl.ds(a + 1, 1), :] += jnp.sum(sum1, axis=0, keepdims=True)

        each_duo(p, offset, duo)
        part = lax.dot_general(
            g_ref[...].astype(BF16), right, (((1,), (1,)), ((), ())), preferred_element_type=F32)
        lad_ref[p] += jnp.where(live, part, 0.0)
        return offset + rows_of(half_width(p))

    lax.fori_loop(0, npair, fold, jnp.int32(0))

    @pl.when(step == pl.num_programs(0) - 1)
    def _():
        out_ref[...] = jnp.zeros_like(out_ref)
        for p in range(npair):
            out_ref[:, p, 0:depth] = lad_ref[p]


def terms(left, right, amplitudes, pair_widths, core_matrix):
    npair, depth, rows = left.shape
    cols = core_matrix.shape[1]
    tile = TILE if cols % TILE == 0 else cols
    most = npair * 4 * depth * (depth // 8 + 1)
    most = -(-most // CHUNK) * CHUNK
    padded = -(-npair // 8) * 8
    return pl.pallas_call(
        term_kernel,
        out_shape=jax.ShapeDtypeStruct((depth, padded, 128), F32),
        grid_spec=pltpu.PrefetchScalarGridSpec(
            num_scalar_prefetch=1,
            grid=(cols // tile,),
            in_specs=[
                pl.BlockSpec((npair, depth, rows), lambda j, w: (0, 0, 0), pipeline_mode=pl.Buffered(1)),
                pl.BlockSpec((npair, depth, depth), lambda j, w: (0, 0, 0), pipeline_mode=pl.Buffered(1)),
                pl.BlockSpec((npair, depth, tile), lambda j, w: (0, 0, j)),
                pl.BlockSpec((rows, tile), lambda j, w: (0, j)),
            ],
            out_specs=pl.BlockSpec((depth, padded, 128), lambda j, w: (0, 0, 0)),
            scratch_shapes=[
                pltpu.VMEM((most, rows), BF16),
                pltpu.VMEM((depth, rows), F32),
                pltpu.VMEM((most, tile), F32),
                pltpu.VMEM((depth, tile), F32),
                pltpu.VMEM((depth, tile), F32),
                pltpu.VMEM((npair, depth, depth), F32),
            ]),
        compiler_params=pltpu.CompilerParams(dimension_semantics=("arbitrary",), vmem_limit_bytes=60 << 20),
        name="terms",
    )(pair_widths, left, amplitudes, right, core_matrix)


def settle_kernel(npart, ngrow, ngcol, npair, plan_ref, lad_ref, out_ref, held, send_sem, recv_sem):
    x, g, c = lax.axis_index("pair"), lax.axis_index("grow"), lax.axis_index("gcol")
    inner = ngrow * ngcol
    count = npart * inner
    me = x * inner + g * ngcol + c
    depth = lad_ref.shape[0]
    share = depth // inner

    def place(k):
        other = lax.rem(me + k, count)
        spot = lax.rem(other, inner)
        return (lax.div(other, inner), lax.div(spot, ngcol), lax.rem(spot, ngcol)), spot

    barrier = pltpu.get_barrier_semaphore()

    def greet(k, carry):
        pl.semaphore_signal(barrier, inc=1, device_id=place(k)[0], device_id_type=MESH)
        return carry

    lax.fori_loop(1, count, greet, 0)
    pl.semaphore_wait(barrier, count - 1)

    def copy(k):
        device, spot = place(k)
        return pltpu.make_async_remote_copy(
            src_ref=lad_ref.at[pl.ds(spot * share, share)], dst_ref=held.at[me], send_sem=send_sem.at[k],
            recv_sem=recv_sem.at[me], device_id=device, device_id_type=MESH)

    def send(k, carry):
        copy(k).start()
        return carry

    lax.fori_loop(1, count, send, 0)
    held[me] = lad_ref[pl.ds(lax.rem(me, inner) * share, share)]

    def finish(k, carry):
        other = lax.rem(me + k, count)
        device, spot = place(k)
        pltpu.make_async_remote_copy(
            src_ref=lad_ref.at[pl.ds(spot * share, share)], dst_ref=held.at[other], send_sem=send_sem.at[k],
            recv_sem=recv_sem.at[other], device_id=device, device_id_type=MESH).wait_recv()
        copy(k).wait_send()
        return carry

    lax.fori_loop(1, count, finish, 0)

    slots = out_ref.shape[1]
    done = [jnp.zeros(out_ref.shape[2:], F32) for _ in range(share * slots)]
    for part in range(npart):
        summed = jnp.sum(held[part * inner : (part + 1) * inner], axis=0)
        for p in range(npair):
            for s in range(slots):
                hit = plan_ref[s] == part * npair + p
                for r in range(share):
                    done[r * slots + s] = jnp.where(hit, summed[r, p], done[r * slots + s])
    for r in range(share):
        for s in range(slots):
            out_ref[r, s] = done[r * slots + s]


def settle(lad, plan, mesh_shape):
    npart, ngrow, ngcol = mesh_shape
    count = npart * ngrow * ngcol
    depth, padded, lanes = lad.shape
    share = depth // (ngrow * ngcol)
    npair = plan.shape[0]
    out = pl.pallas_call(
        functools.partial(settle_kernel, npart, ngrow, ngcol, npair),
        out_shape=jax.ShapeDtypeStruct((share, npair, lanes), F32),
        in_specs=[pl.BlockSpec(memory_space=pltpu.SMEM), pl.BlockSpec(memory_space=pltpu.VMEM)],
        out_specs=pl.BlockSpec(memory_space=pltpu.VMEM),
        scratch_shapes=[
            pltpu.VMEM((count, share, padded, lanes), F32),
            pltpu.SemaphoreType.DMA((count,)),
            pltpu.SemaphoreType.DMA((count,)),
        ],
        compiler_params=pltpu.CompilerParams(collective_id=1, has_side_effects=True),
        name="settle",
    )(plan, lad)
    return jnp.swapaxes(out[:, :, :depth], 0, 1).reshape(npair, share * depth)


def gather(panels, ngrow, ngcol):
    npair, depth, piece = panels.shape
    return pl.pallas_call(
        functools.partial(gather_kernel, ngrow, ngcol),
        out_shape=(
            jax.ShapeDtypeStruct((npair, depth, piece * ngcol), panels.dtype),
            jax.ShapeDtypeStruct((npair, depth, piece * ngrow), panels.dtype),
        ),
        in_specs=[pl.BlockSpec(memory_space=pltpu.VMEM)],
        out_specs=[pl.BlockSpec(memory_space=pl.ANY)] * 2,
        scratch_shapes=[
            pltpu.SemaphoreType.DMA((ngcol,)),
            pltpu.SemaphoreType.DMA((ngcol,)),
            pltpu.SemaphoreType.DMA((ngrow,)),
            pltpu.SemaphoreType.DMA((ngrow,)),
            pltpu.SemaphoreType.DMA((2,)),
        ],
        compiler_params=pltpu.CompilerParams(collective_id=0, has_side_effects=True),
        name="gather",
    )(panels)


def solution(mesh):
    shape = (mesh.shape["pair"], mesh.shape["grow"], mesh.shape["gcol"])

    def local(core_matrix, pair_panels, amplitudes, pair_widths, batch_plan):
        left, right = gather(pair_panels, shape[1], shape[2])
        lad = terms(left, right, amplitudes, pair_widths, core_matrix)
        return settle(lad, batch_plan, shape)

    in_specs = (
        P("grow", "gcol"),
        P("pair", None, ("grow", "gcol")),
        P("pair", None, None),
        P("pair"),
        P("pair"),
    )
    out_specs = P("pair", ("grow", "gcol"))
    return jax.shard_map(local, mesh=mesh, in_specs=in_specs, out_specs=out_specs, check_vma=False)
```

```python
import functools

import jax
import jax.numpy as jnp
from jax import lax
from jax.experimental import pallas as pl
from jax.experimental.pallas import tpu as pltpu
from jax.sharding import PartitionSpec as P

MESH = pl.DeviceIdType.MESH
TILE = 1024
CHUNK = 256
F32 = jnp.float32
BF16 = jnp.bfloat16


def gather_kernel(ngrow, ngcol, panel_ref, left_ref, right_ref, send_sem, recv_sem, tree_send, tree_recv, own_sem):
    x, g, c = lax.axis_index("pair"), lax.axis_index("grow"), lax.axis_index("gcol")
    piece = panel_ref.shape[2]
    bits = ngrow.bit_length() - 1
    root = lax.div(c * ngrow, ngcol)
    first = lax.rem(c * ngrow, ngcol)

    def bit(value, b):
        return lax.rem(lax.div(value, 1 << b), 2)

    def flip(b):
        return g + (1 << b) * (1 - 2 * bit(g, b))

    differ = [lax.rem(bit(g, b) + bit(root, b), 2) for b in range(bits)]
    before = [jnp.int32(0)]
    for b in range(bits):
        before.append(before[-1] + differ[b])
    is_root = before[bits] == 0

    barrier = pltpu.get_barrier_semaphore()

    def greet(device):
        pl.semaphore_signal(barrier, inc=1, device_id=device, device_id_type=MESH)

    @pl.when(c > 0)
    def _():
        greet((x, g, c - 1))

    @pl.when(c < ngcol - 1)
    def _():
        greet((x, g, c + 1))

    expected = jnp.where(c > 0, 1, 0) + jnp.where(c < ngcol - 1, 1, 0)
    for b in range(bits):
        expected += jnp.where(before[b] == 0, 1, 0)

        @pl.when(before[b] == 0)
        def _():
            greet((x, flip(b), c))

    pl.semaphore_wait(barrier, expected)

    def spot(ref, at):
        return ref.at[:, :, pl.ds(pl.multiple_of(at * piece, 128), piece)]

    def hop(way, at, own):
        return pltpu.make_async_remote_copy(
            src_ref=panel_ref if own else spot(left_ref, at), dst_ref=spot(left_ref, at),
            send_sem=send_sem.at[way, at], recv_sem=recv_sem.at[at],
            device_id=(x, g, c + 1 - 2 * way), device_id_type=MESH)

    def branch(b, j, at):
        return pltpu.make_async_remote_copy(
            src_ref=spot(right_ref, j) if at is None else spot(left_ref, at), dst_ref=spot(right_ref, j),
            send_sem=tree_send.at[b, j], recv_sem=tree_recv.at[j],
            device_id=(x, flip(b), c), device_id_type=MESH)

    def own_right(j, at):
        return pltpu.make_async_copy(spot(left_ref, at), spot(right_ref, j), own_sem.at[1 + j])

    def arrivals(s):
        found = [(c - s, c - s >= 0)]
        return found if s == 0 else found + [(c + s, c + s <= ngcol - 1)]

    def inside(at, valid):
        return jnp.logical_and(valid, jnp.logical_and(at >= first, at < first + ngrow))

    own_left = pltpu.make_async_copy(panel_ref, spot(left_ref, c), own_sem.at[0])

    def ways(s):
        return (0, c - s, jnp.logical_and(c - s >= 0, c < ngcol - 1)), (1, c + s, jnp.logical_and(c + s <= ngcol - 1, c > 0))

    def line(s):
        if s > 0:
            for way, (at, valid) in enumerate(arrivals(s)):
                @pl.when(valid)
                def _(way=way, at=at):
                    hop(way, at, False).wait_recv()

        for way, at, valid in ways(s):
            if s < ngcol - 1:
                @pl.when(valid)
                def _(way=way, at=at):
                    hop(way, at, s == 0).start()

        if s == 0:
            own_left.start()
            own_left.wait()

        for at, valid in arrivals(s):
            @pl.when(jnp.logical_and(is_root, inside(at, valid)))
            def _(at=at):
                for b in reversed(range(bits)):
                    branch(b, at - first, at).start()
                own_right(at - first, at).start()

    def tree(s):
        for at, valid in arrivals(s):
            here = inside(at, valid)

            @pl.when(jnp.logical_and(jnp.logical_not(is_root), here))
            def _(at=at):
                branch(0, at - first, None).wait_recv()
                for b in range(bits):
                    @pl.when(before[b + 1] == 0)
                    def _(b=b):
                        branch(b, at - first, None).start()

    for s in range(ngcol):
        line(s)
        if s > 0:
            tree(s - 1)
    tree(ngcol - 1)

    for s in range(ngcol):
        for way, at, valid in ways(s):
            if s < ngcol - 1:
                @pl.when(valid)
                def _(way=way, at=at):
                    hop(way, at, s == 0).wait_send()

        for at, valid in arrivals(s):
            here = inside(at, valid)

            @pl.when(jnp.logical_and(is_root, here))
            def _(at=at):
                own_right(at - first, at).wait()

            for b in range(bits):
                @pl.when(jnp.logical_and(before[b + 1] == 0, here))
                def _(at=at, b=b):
                    branch(b, at - first, None).wait_send()


def term_kernel(widths, left_ref, amps_ref, right_ref, core_ref, out_ref, y_ref, x_ref, v_ref, p_ref, g_ref, lad_ref):
    step = pl.program_id(0)
    npair, depth, _ = left_ref.shape
    groups = depth // 8

    def half_width(p):
        return lax.div(widths[p] + 1, 2)

    def rows_of(count):
        full = lax.div(count, 4)
        return 16 * (2 * full * (full + 1) + lax.rem(count, 4) * (full + 1))

    def each_duo(p, offset, body):
        count = half_width(p)
        for group in range(groups):
            low = 4 * group

            def run(duo, carry, group=group, low=low):
                base = offset + 16 * (2 * group * (group + 1) + (duo - low) * (group + 1))
                body(group, 2 * duo, pl.multiple_of(base, 16))
                return carry

            lax.fori_loop(low, jnp.clip(count, low, low + 4), run, 0)

    @pl.when(step == 0)
    def _():
        lad_ref[...] = jnp.zeros_like(lad_ref)

        def build(p, offset):
            x_ref[...] = left_ref[p].astype(F32)

            def duo(group, a, base):
                first, second = x_ref[pl.ds(a, 1), :], x_ref[pl.ds(a + 1, 1), :]
                for other in range(group + 1):
                    block = x_ref[8 * other : 8 * other + 8, :]
                    both = jnp.concatenate([first * block, second * block], axis=0)
                    y_ref[pl.ds(base + 16 * other, 16), :] = both.astype(BF16)

            each_duo(p, offset, duo)
            return offset + rows_of(half_width(p))

        lax.fori_loop(0, npair, build, jnp.int32(0))

    total = jnp.int32(0)
    for p in range(npair):
        total += rows_of(half_width(p))

    def multiply(size, i, carry):
        rows = pl.ds(pl.multiple_of(i * size, size), size)
        v_ref[rows, :] = jnp.dot(y_ref[rows, :], core_ref[...], preferred_element_type=F32)
        return carry

    pieces = lax.div(total + CHUNK - 1, CHUNK)
    wholes = lax.div(pieces, 2)
    lax.fori_loop(0, wholes, functools.partial(multiply, 2 * CHUNK), 0)
    lax.fori_loop(2 * wholes, pieces, functools.partial(multiply, CHUNK), 0)

    def fold(p, offset):
        width = widths[p]
        live = jnp.logical_and(
            lax.broadcasted_iota(jnp.int32, (depth, depth), 0) < width,
            lax.broadcasted_iota(jnp.int32, (depth, depth), 1) < width)
        masked = jnp.where(live, amps_ref[p].astype(F32), 0.0).astype(BF16)
        right = right_ref[p]
        p_ref[...] = jnp.dot(masked, right, preferred_element_type=F32).astype(BF16).astype(F32)
        g_ref[...] = jnp.zeros_like(g_ref)

        def duo(group, a, base):
            first, second = p_ref[pl.ds(a, 1), :], p_ref[pl.ds(a + 1, 1), :]
            sum0 = sum1 = None
            for other in range(group + 1):
                upper = v_ref[pl.ds(base + 16 * other, 8), :]
                lower = v_ref[pl.ds(base + 16 * other + 8, 8), :]
                proj = p_ref[8 * other : 8 * other + 8, :]
                sum0 = upper * proj if sum0 is None else sum0 + upper * proj
                sum1 = lower * proj if sum1 is None else sum1 + lower * proj
                if other < group:
                    g_ref[8 * other : 8 * other + 8, :] += upper * first + lower * second
            g_ref[pl.ds(a, 1), :] += jnp.sum(sum0, axis=0, keepdims=True)
            g_ref[pl.ds(a + 1, 1), :] += jnp.sum(sum1, axis=0, keepdims=True)

        each_duo(p, offset, duo)
        part = lax.dot_general(
            g_ref[...].astype(BF16), right, (((1,), (1,)), ((), ())), preferred_element_type=F32)
        lad_ref[p] += jnp.where(live, part, 0.0)
        return offset + rows_of(half_width(p))

    lax.fori_loop(0, npair, fold, jnp.int32(0))

    @pl.when(step == pl.num_programs(0) - 1)
    def _():
        out_ref[...] = jnp.zeros_like(out_ref)
        ngrow, ngcol, padded, lanes = out_ref.shape
        share = depth // (ngrow * ngcol)
        for p in range(npair):
            parts = [lad_ref[p, pl.ds(r, ngrow * ngcol, stride=share), :] for r in range(share)]
            row = parts[0] if share == 1 else jnp.concatenate(parts, axis=1)
            for at in range(ngrow):
                out_ref[at, :, p, 0 : share * depth] = row[at * ngcol : (at + 1) * ngcol]


def terms(left, right, amplitudes, pair_widths, core_matrix, ngrow, ngcol):
    npair, depth, rows = left.shape
    cols = core_matrix.shape[1]
    tile = TILE if cols % TILE == 0 else cols
    most = npair * 4 * depth * (depth // 8 + 1)
    most = -(-most // CHUNK) * CHUNK
    padded = -(-npair // 8) * 8
    return pl.pallas_call(
        term_kernel,
        out_shape=jax.ShapeDtypeStruct((ngrow, ngcol, padded, 128), F32),
        grid_spec=pltpu.PrefetchScalarGridSpec(
            num_scalar_prefetch=1,
            grid=(cols // tile,),
            in_specs=[
                pl.BlockSpec((npair, depth, rows), lambda j, w: (0, 0, 0), pipeline_mode=pl.Buffered(1)),
                pl.BlockSpec((npair, depth, depth), lambda j, w: (0, 0, 0), pipeline_mode=pl.Buffered(1)),
                pl.BlockSpec((npair, depth, tile), lambda j, w: (0, 0, j)),
                pl.BlockSpec((rows, tile), lambda j, w: (0, j)),
            ],
            out_specs=pl.BlockSpec((ngrow, ngcol, padded, 128), lambda j, w: (0, 0, 0, 0)),
            scratch_shapes=[
                pltpu.VMEM((most, rows), BF16),
                pltpu.VMEM((depth, rows), F32),
                pltpu.VMEM((most, tile), F32),
                pltpu.VMEM((depth, tile), F32),
                pltpu.VMEM((depth, tile), F32),
                pltpu.VMEM((npair, depth, depth), F32),
            ]),
        compiler_params=pltpu.CompilerParams(dimension_semantics=("arbitrary",), vmem_limit_bytes=60 << 20),
        name="terms",
    )(pair_widths, left, amplitudes, right, core_matrix)


def settle_kernel(npart, ngrow, ngcol, npair, plan_ref, lad_ref, out_ref, row_ref, sum_ref, held_ref, send_sem, recv_sem, wide_send, wide_recv):
    x, g, c = lax.axis_index("pair"), lax.axis_index("grow"), lax.axis_index("gcol")
    count = npart * ngrow
    me = x * ngrow + g

    def seat(k):
        other = lax.rem(me + k, count)
        return other, lax.div(other, ngrow), lax.rem(other, ngrow)

    barrier = pltpu.get_barrier_semaphore()

    def greet(device):
        pl.semaphore_signal(barrier, inc=1, device_id=device, device_id_type=MESH)

    for k in range(1, ngcol):
        greet((x, g, lax.rem(c + k, ngcol)))
    for k in range(1, count):
        _, xo, go = seat(k)
        greet((xo, go, c))
    pl.semaphore_wait(barrier, ngcol - 1 + count - 1)

    def near(k, at):
        to = lax.rem(c + k, ngcol)
        return pltpu.make_async_remote_copy(
            src_ref=lad_ref.at[:, to], dst_ref=row_ref.at[at], send_sem=send_sem.at[k], recv_sem=recv_sem.at[at],
            device_id=(x, g, to), device_id_type=MESH)

    def wide(k, at):
        _, xo, go = seat(k)
        return pltpu.make_async_remote_copy(
            src_ref=sum_ref.at[go], dst_ref=held_ref.at[at], send_sem=wide_send.at[k], recv_sem=wide_recv.at[at],
            device_id=(xo, go, c), device_id_type=MESH)

    for k in range(1, ngcol):
        near(k, c).start()
    total = lad_ref[:, c]
    for k in range(1, ngcol):
        source = lax.rem(c + k, ngcol)
        near(k, source).wait_recv()
        total = total + row_ref[source]
    sum_ref[...] = total
    for k in range(1, count):
        wide(k, me).start()
    held_ref[me] = sum_ref[g]
    for k in range(1, count):
        wide(k, seat(k)[0]).wait_recv()
    slots = out_ref.shape[0]
    done = [jnp.zeros(out_ref.shape[1:], F32) for _ in range(slots)]
    for part in range(npart):
        summed = jnp.sum(held_ref[part * ngrow : (part + 1) * ngrow], axis=0)
        for p in range(npair):
            for s in range(slots):
                done[s] = jnp.where(plan_ref[s] == part * npair + p, summed[p], done[s])
    for s in range(slots):
        out_ref[s] = done[s]
    for k in range(1, ngcol):
        near(k, c).wait_send()
    for k in range(1, count):
        wide(k, me).wait_send()


def settle(lad, plan, mesh_shape):
    npart, ngrow, ngcol = mesh_shape
    count = npart * ngrow
    _, _, padded, lanes = lad.shape
    npair = plan.shape[0]
    return pl.pallas_call(
        functools.partial(settle_kernel, npart, ngrow, ngcol, npair),
        out_shape=jax.ShapeDtypeStruct((npair, lanes), F32),
        in_specs=[pl.BlockSpec(memory_space=pltpu.SMEM), pl.BlockSpec(memory_space=pltpu.VMEM)],
        out_specs=pl.BlockSpec(memory_space=pltpu.VMEM),
        scratch_shapes=[
            pltpu.VMEM((ngcol, ngrow, padded, lanes), F32),
            pltpu.VMEM((ngrow, padded, lanes), F32),
            pltpu.VMEM((count, padded, lanes), F32),
            pltpu.SemaphoreType.DMA((ngcol,)),
            pltpu.SemaphoreType.DMA((ngcol,)),
            pltpu.SemaphoreType.DMA((count,)),
            pltpu.SemaphoreType.DMA((count,)),
        ],
        compiler_params=pltpu.CompilerParams(collective_id=1, has_side_effects=True),
        name="settle",
    )(plan, lad)


def gather(panels, ngrow, ngcol):
    npair, depth, piece = panels.shape
    return pl.pallas_call(
        functools.partial(gather_kernel, ngrow, ngcol),
        out_shape=(
            jax.ShapeDtypeStruct((npair, depth, piece * ngcol), panels.dtype),
            jax.ShapeDtypeStruct((npair, depth, piece * ngrow), panels.dtype),
        ),
        in_specs=[pl.BlockSpec(memory_space=pltpu.VMEM)],
        out_specs=[pl.BlockSpec(memory_space=pltpu.VMEM)] * 2,
        scratch_shapes=[
            pltpu.SemaphoreType.DMA((2, ngcol)),
            pltpu.SemaphoreType.DMA((ngcol,)),
            pltpu.SemaphoreType.DMA((ngrow.bit_length() - 1, ngrow)),
            pltpu.SemaphoreType.DMA((ngrow,)),
            pltpu.SemaphoreType.DMA((1 + ngrow,)),
        ],
        compiler_params=pltpu.CompilerParams(collective_id=0, has_side_effects=True),
        name="gather",
    )(panels)


def solution(mesh):
    shape = (mesh.shape["pair"], mesh.shape["grow"], mesh.shape["gcol"])

    def local(core_matrix, pair_panels, amplitudes, pair_widths, batch_plan):
        left, right = gather(pair_panels, shape[1], shape[2])
        lad = terms(left, right, amplitudes, pair_widths, core_matrix, shape[1], shape[2])
        width = amplitudes.shape[1] ** 2 // (shape[1] * shape[2])
        return settle(lad, batch_plan, shape)[:, :width]

    in_specs = (
        P("grow", "gcol"),
        P("pair", None, ("grow", "gcol")),
        P("pair", None, None),
        P("pair"),
        P("pair"),
    )
    out_specs = P("pair", ("grow", "gcol"))
    return jax.shard_map(local, mesh=mesh, in_specs=in_specs, out_specs=out_specs, check_vma=False)
```

```python
import functools

import jax
import jax.numpy as jnp
from jax import lax
from jax.experimental import pallas as pl
from jax.experimental.pallas import tpu as pltpu
from jax.sharding import PartitionSpec as P

MESH = pl.DeviceIdType.MESH
TILE = 1024
CHUNK = 384
F32 = jnp.float32
BF16 = jnp.bfloat16


def gather_kernel(ngrow, ngcol, panel_ref, left_ref, right_ref, send_sem, recv_sem, tree_send, tree_recv, own_sem):
    x, g, c = lax.axis_index("pair"), lax.axis_index("grow"), lax.axis_index("gcol")
    piece = panel_ref.shape[2]
    bits = ngrow.bit_length() - 1
    root = lax.div(c * ngrow, ngcol)
    first = lax.rem(c * ngrow, ngcol)

    def bit(value, b):
        return lax.rem(lax.div(value, 1 << b), 2)

    def flip(b):
        return g + (1 << b) * (1 - 2 * bit(g, b))

    differ = [lax.rem(bit(g, b) + bit(root, b), 2) for b in range(bits)]
    before = [jnp.int32(0)]
    for b in range(bits):
        before.append(before[-1] + differ[b])
    is_root = before[bits] == 0

    barrier = pltpu.get_barrier_semaphore()

    def greet(device):
        pl.semaphore_signal(barrier, inc=1, device_id=device, device_id_type=MESH)

    @pl.when(c > 0)
    def _():
        greet((x, g, c - 1))

    @pl.when(c < ngcol - 1)
    def _():
        greet((x, g, c + 1))

    expected = jnp.where(c > 0, 1, 0) + jnp.where(c < ngcol - 1, 1, 0)
    for b in range(bits):
        expected += jnp.where(before[b] == 0, 1, 0)

        @pl.when(before[b] == 0)
        def _():
            greet((x, flip(b), c))

    pl.semaphore_wait(barrier, expected)

    def spot(ref, at):
        return ref.at[:, :, pl.ds(pl.multiple_of(at * piece, 128), piece)]

    def hop(way, at, own):
        return pltpu.make_async_remote_copy(
            src_ref=panel_ref if own else spot(left_ref, at), dst_ref=spot(left_ref, at),
            send_sem=send_sem.at[way, at], recv_sem=recv_sem.at[at],
            device_id=(x, g, c + 1 - 2 * way), device_id_type=MESH)

    def branch(b, j, at):
        return pltpu.make_async_remote_copy(
            src_ref=spot(right_ref, j) if at is None else spot(left_ref, at), dst_ref=spot(right_ref, j),
            send_sem=tree_send.at[b, j], recv_sem=tree_recv.at[j],
            device_id=(x, flip(b), c), device_id_type=MESH)

    def own_right(j, at):
        return pltpu.make_async_copy(spot(left_ref, at), spot(right_ref, j), own_sem.at[1 + j])

    def arrivals(s):
        found = [(c - s, c - s >= 0)]
        return found if s == 0 else found + [(c + s, c + s <= ngcol - 1)]

    def inside(at, valid):
        return jnp.logical_and(valid, jnp.logical_and(at >= first, at < first + ngrow))

    own_left = pltpu.make_async_copy(panel_ref, spot(left_ref, c), own_sem.at[0])

    def ways(s):
        return (0, c - s, jnp.logical_and(c - s >= 0, c < ngcol - 1)), (1, c + s, jnp.logical_and(c + s <= ngcol - 1, c > 0))

    def line(s):
        if s > 0:
            for way, (at, valid) in enumerate(arrivals(s)):
                @pl.when(valid)
                def _(way=way, at=at):
                    hop(way, at, False).wait_recv()

        for way, at, valid in ways(s):
            if s < ngcol - 1:
                @pl.when(valid)
                def _(way=way, at=at):
                    hop(way, at, s == 0).start()

        if s == 0:
            own_left.start()
            own_left.wait()

        for at, valid in arrivals(s):
            @pl.when(jnp.logical_and(is_root, inside(at, valid)))
            def _(at=at):
                for b in reversed(range(bits)):
                    branch(b, at - first, at).start()
                own_right(at - first, at).start()

    def tree(s):
        for at, valid in arrivals(s):
            here = inside(at, valid)

            @pl.when(jnp.logical_and(jnp.logical_not(is_root), here))
            def _(at=at):
                branch(0, at - first, None).wait_recv()
                for b in range(bits):
                    @pl.when(before[b + 1] == 0)
                    def _(b=b):
                        branch(b, at - first, None).start()

    for s in range(ngcol):
        line(s)
        if s > 0:
            tree(s - 1)
    tree(ngcol - 1)

    for s in range(ngcol):
        for way, at, valid in ways(s):
            if s < ngcol - 1:
                @pl.when(valid)
                def _(way=way, at=at):
                    hop(way, at, s == 0).wait_send()

        for at, valid in arrivals(s):
            here = inside(at, valid)

            @pl.when(jnp.logical_and(is_root, here))
            def _(at=at):
                own_right(at - first, at).wait()

            for b in range(bits):
                @pl.when(jnp.logical_and(before[b + 1] == 0, here))
                def _(at=at, b=b):
                    branch(b, at - first, None).wait_send()


def term_kernel(
    widths, left_ref, amps_ref, right_ref, core_ref, out_ref,
    y_ref, x_ref, even_ref, odd_ref, p_ref, own_ref, other_ref, lad_ref, first_ref, second_ref, cross_ref,
):
    step = pl.program_id(0)
    npair, depth, _ = left_ref.shape
    groups = depth // 8
    units = CHUNK // 16

    def half_width(p):
        return lax.div(widths[p] + 1, 2)

    def rows_of(count):
        full = lax.div(count, 4)
        return 16 * (2 * full * (full + 1) + lax.rem(count, 4) * (full + 1))

    total = jnp.int32(0)
    for p in range(npair):
        total += rows_of(half_width(p))
    chunks = lax.div(total + CHUNK - 1, CHUNK)

    @pl.when(step == 0)
    def _():
        lad_ref[...] = jnp.zeros_like(lad_ref)

        def build(p, offset):
            x_ref[...] = left_ref[p].astype(F32)
            count = half_width(p)
            for group in range(groups):
                low = 4 * group

                def duo(k, carry, group=group, low=low):
                    a = 2 * k
                    base = offset + 16 * (2 * group * (group + 1) + (k - low) * (group + 1))
                    base = pl.multiple_of(base, 16)
                    unit = lax.div(base, 16)
                    upper, lower = x_ref[pl.ds(a, 1), :], x_ref[pl.ds(a + 1, 1), :]
                    for other in range(group + 1):
                        block = x_ref[8 * other : 8 * other + 8, :]
                        both = jnp.concatenate([upper * block, lower * block], axis=0)
                        y_ref[pl.ds(base + 16 * other, 16), :] = both.astype(BF16)
                        first_ref[unit + other] = p * depth + a
                        second_ref[unit + other] = p * depth + 8 * other
                        cross_ref[unit + other] = jnp.float32(1.0 if other < group else 0.0)
                    return carry

                lax.fori_loop(low, jnp.clip(count, low, low + 4), duo, 0)
            return offset + rows_of(count)

        lax.fori_loop(0, npair, build, jnp.int32(0))

        def blank(unit, carry):
            y_ref[pl.ds(pl.multiple_of(unit * 16, 16), 16), :] = jnp.zeros((16, y_ref.shape[1]), BF16)
            first_ref[unit] = jnp.int32(0)
            second_ref[unit] = jnp.int32(0)
            cross_ref[unit] = jnp.float32(0.0)
            return carry

        lax.fori_loop(lax.div(total, 16), chunks * units, blank, 0)

    def live(p):
        return jnp.logical_and(
            lax.broadcasted_iota(jnp.int32, (depth, depth), 0) < widths[p],
            lax.broadcasted_iota(jnp.int32, (depth, depth), 1) < widths[p])

    for p in range(npair):
        masked = jnp.where(live(p), amps_ref[p].astype(F32), 0.0).astype(BF16)
        p_ref[p * depth : (p + 1) * depth, :] = (
            jnp.dot(masked, right_ref[p], preferred_element_type=F32).astype(BF16).astype(F32))
    own_ref[...] = jnp.zeros_like(own_ref)
    other_ref[...] = jnp.zeros_like(other_ref)

    def multiply(i, into_ref):
        rows = pl.ds(pl.multiple_of(i * CHUNK, CHUNK), CHUNK)
        into_ref[...] = jnp.dot(y_ref[rows, :], core_ref[...], preferred_element_type=F32)

    def fold(i, from_ref):
        for k in range(units):
            unit = i * units + k
            a = first_ref[unit]
            c = pl.multiple_of(second_ref[unit], 8)
            cross = cross_ref[unit]
            upper = from_ref[16 * k : 16 * k + 8, :]
            lower = from_ref[16 * k + 8 : 16 * k + 16, :]
            proj = p_ref[pl.ds(c, 8), :]
            own_ref[pl.ds(a, 1), :] += jnp.sum(upper * proj, axis=0, keepdims=True)
            own_ref[pl.ds(a + 1, 1), :] += jnp.sum(lower * proj, axis=0, keepdims=True)
            other_ref[pl.ds(c, 8), :] += (
                upper * (p_ref[pl.ds(a, 1), :] * cross) + lower * (p_ref[pl.ds(a + 1, 1), :] * cross))

    multiply(0, even_ref)

    def both(i, carry):
        multiply(2 * i + 1, odd_ref)
        fold(2 * i, even_ref)
        multiply(2 * i + 2, even_ref)
        fold(2 * i + 1, odd_ref)
        return carry

    rounds = lax.div(chunks - 1, 2)
    lax.fori_loop(0, rounds, both, 0)

    @pl.when(lax.rem(chunks, 2) == 1)
    def _():
        fold(chunks - 1, even_ref)

    @pl.when(lax.rem(chunks, 2) == 0)
    def _():
        multiply(chunks - 1, odd_ref)
        fold(chunks - 2, even_ref)
        fold(chunks - 1, odd_ref)

    for p in range(npair):
        rows = slice(p * depth, (p + 1) * depth)
        whole = (own_ref[rows, :] + other_ref[rows, :]).astype(BF16)
        part = lax.dot_general(whole, right_ref[p], (((1,), (1,)), ((), ())), preferred_element_type=F32)
        lad_ref[p] += jnp.where(live(p), part, 0.0)

    @pl.when(step == pl.num_programs(0) - 1)
    def _():
        out_ref[...] = jnp.zeros_like(out_ref)
        ngrow, ngcol, padded, lanes = out_ref.shape
        share = depth // (ngrow * ngcol)
        for p in range(npair):
            parts = [lad_ref[p, pl.ds(r, ngrow * ngcol, stride=share), :] for r in range(share)]
            row = parts[0] if share == 1 else jnp.concatenate(parts, axis=1)
            for at in range(ngrow):
                out_ref[at, :, p, 0 : share * depth] = row[at * ngcol : (at + 1) * ngcol]


def terms(left, right, amplitudes, pair_widths, core_matrix, ngrow, ngcol):
    npair, depth, rows = left.shape
    cols = core_matrix.shape[1]
    tile = TILE if cols % TILE == 0 else cols
    most = npair * 4 * depth * (depth // 8 + 1)
    most = -(-most // CHUNK) * CHUNK
    padded = -(-npair // 8) * 8
    return pl.pallas_call(
        term_kernel,
        out_shape=jax.ShapeDtypeStruct((ngrow, ngcol, padded, 128), F32),
        grid_spec=pltpu.PrefetchScalarGridSpec(
            num_scalar_prefetch=1,
            grid=(cols // tile,),
            in_specs=[
                pl.BlockSpec((npair, depth, rows), lambda j, w: (0, 0, 0), pipeline_mode=pl.Buffered(1)),
                pl.BlockSpec((npair, depth, depth), lambda j, w: (0, 0, 0), pipeline_mode=pl.Buffered(1)),
                pl.BlockSpec((npair, depth, tile), lambda j, w: (0, 0, j)),
                pl.BlockSpec((rows, tile), lambda j, w: (0, j)),
            ],
            out_specs=pl.BlockSpec((ngrow, ngcol, padded, 128), lambda j, w: (0, 0, 0, 0)),
            scratch_shapes=[
                pltpu.VMEM((most, rows), BF16),
                pltpu.VMEM((depth, rows), F32),
                pltpu.VMEM((CHUNK, tile), F32),
                pltpu.VMEM((CHUNK, tile), F32),
                pltpu.VMEM((npair * depth, tile), F32),
                pltpu.VMEM((npair * depth, tile), F32),
                pltpu.VMEM((npair * depth, tile), F32),
                pltpu.VMEM((npair, depth, depth), F32),
                pltpu.SMEM((most // 16,), jnp.int32),
                pltpu.SMEM((most // 16,), jnp.int32),
                pltpu.SMEM((most // 16,), F32),
            ]),
        compiler_params=pltpu.CompilerParams(dimension_semantics=("arbitrary",), vmem_limit_bytes=60 << 20),
        name="terms",
    )(pair_widths, left, amplitudes, right, core_matrix)


def settle_kernel(npart, ngrow, ngcol, npair, plan_ref, lad_ref, out_ref, row_ref, sum_ref, held_ref, send_sem, recv_sem, wide_send, wide_recv):
    x, g, c = lax.axis_index("pair"), lax.axis_index("grow"), lax.axis_index("gcol")
    count = npart * ngrow
    me = x * ngrow + g

    def seat(k):
        other = lax.rem(me + k, count)
        return other, lax.div(other, ngrow), lax.rem(other, ngrow)

    barrier = pltpu.get_barrier_semaphore()

    def greet(device):
        pl.semaphore_signal(barrier, inc=1, device_id=device, device_id_type=MESH)

    for k in range(1, ngcol):
        greet((x, g, lax.rem(c + k, ngcol)))
    for k in range(1, count):
        _, xo, go = seat(k)
        greet((xo, go, c))
    pl.semaphore_wait(barrier, ngcol - 1 + count - 1)

    def near(k, at):
        to = lax.rem(c + k, ngcol)
        return pltpu.make_async_remote_copy(
            src_ref=lad_ref.at[:, to], dst_ref=row_ref.at[at], send_sem=send_sem.at[k], recv_sem=recv_sem.at[at],
            device_id=(x, g, to), device_id_type=MESH)

    def wide(k, at):
        _, xo, go = seat(k)
        return pltpu.make_async_remote_copy(
            src_ref=sum_ref.at[go], dst_ref=held_ref.at[at], send_sem=wide_send.at[k], recv_sem=wide_recv.at[at],
            device_id=(xo, go, c), device_id_type=MESH)

    for k in range(1, ngcol):
        near(k, c).start()
    total = lad_ref[:, c]
    for k in range(1, ngcol):
        source = lax.rem(c + k, ngcol)
        near(k, source).wait_recv()
        total = total + row_ref[source]
    sum_ref[...] = total
    for k in range(1, count):
        wide(k, me).start()
    held_ref[me] = sum_ref[g]
    for k in range(1, count):
        wide(k, seat(k)[0]).wait_recv()
    slots = out_ref.shape[0]
    done = [jnp.zeros(out_ref.shape[1:], F32) for _ in range(slots)]
    for part in range(npart):
        summed = jnp.sum(held_ref[part * ngrow : (part + 1) * ngrow], axis=0)
        for p in range(npair):
            for s in range(slots):
                done[s] = jnp.where(plan_ref[s] == part * npair + p, summed[p], done[s])
    for s in range(slots):
        out_ref[s] = done[s]
    for k in range(1, ngcol):
        near(k, c).wait_send()
    for k in range(1, count):
        wide(k, me).wait_send()


def settle(lad, plan, mesh_shape):
    npart, ngrow, ngcol = mesh_shape
    count = npart * ngrow
    _, _, padded, lanes = lad.shape
    npair = plan.shape[0]
    return pl.pallas_call(
        functools.partial(settle_kernel, npart, ngrow, ngcol, npair),
        out_shape=jax.ShapeDtypeStruct((npair, lanes), F32),
        in_specs=[pl.BlockSpec(memory_space=pltpu.SMEM), pl.BlockSpec(memory_space=pltpu.VMEM)],
        out_specs=pl.BlockSpec(memory_space=pltpu.VMEM),
        scratch_shapes=[
            pltpu.VMEM((ngcol, ngrow, padded, lanes), F32),
            pltpu.VMEM((ngrow, padded, lanes), F32),
            pltpu.VMEM((count, padded, lanes), F32),
            pltpu.SemaphoreType.DMA((ngcol,)),
            pltpu.SemaphoreType.DMA((ngcol,)),
            pltpu.SemaphoreType.DMA((count,)),
            pltpu.SemaphoreType.DMA((count,)),
        ],
        compiler_params=pltpu.CompilerParams(collective_id=1, has_side_effects=True),
        name="settle",
    )(plan, lad)


def gather(panels, ngrow, ngcol):
    npair, depth, piece = panels.shape
    return pl.pallas_call(
        functools.partial(gather_kernel, ngrow, ngcol),
        out_shape=(
            jax.ShapeDtypeStruct((npair, depth, piece * ngcol), panels.dtype),
            jax.ShapeDtypeStruct((npair, depth, piece * ngrow), panels.dtype),
        ),
        in_specs=[pl.BlockSpec(memory_space=pltpu.VMEM)],
        out_specs=[pl.BlockSpec(memory_space=pltpu.VMEM)] * 2,
        scratch_shapes=[
            pltpu.SemaphoreType.DMA((2, ngcol)),
            pltpu.SemaphoreType.DMA((ngcol,)),
            pltpu.SemaphoreType.DMA((ngrow.bit_length() - 1, ngrow)),
            pltpu.SemaphoreType.DMA((ngrow,)),
            pltpu.SemaphoreType.DMA((1 + ngrow,)),
        ],
        compiler_params=pltpu.CompilerParams(collective_id=0, has_side_effects=True),
        name="gather",
    )(panels)


def solution(mesh):
    shape = (mesh.shape["pair"], mesh.shape["grow"], mesh.shape["gcol"])

    def local(core_matrix, pair_panels, amplitudes, pair_widths, batch_plan):
        left, right = gather(pair_panels, shape[1], shape[2])
        lad = terms(left, right, amplitudes, pair_widths, core_matrix, shape[1], shape[2])
        width = amplitudes.shape[1] ** 2 // (shape[1] * shape[2])
        return settle(lad, batch_plan, shape)[:, :width]

    in_specs = (
        P("grow", "gcol"),
        P("pair", None, ("grow", "gcol")),
        P("pair", None, None),
        P("pair"),
        P("pair"),
    )
    out_specs = P("pair", ("grow", "gcol"))
    return jax.shard_map(local, mesh=mesh, in_specs=in_specs, out_specs=out_specs, check_vma=False)
```
